32 devices in a mesh: groups: 2 (over x), rows: 16 (over z, y, core).
Axes of the slice: x: 2, y: 2, z: 4, core: 2. Of those that a mesh axis runs over, the one named last changes fastest.
Arguments:
- volume: bfloat16 [32, 128, 8, 512], P(None, ('groups', 'rows')), parts along dimension 1, may hold values from -6 to 6
- fine_first: bfloat16 [3, 3, 3, 32, 32], replicated, may hold values from -0.3125 to 0.3125
- fine_second: bfloat16 [3, 3, 3, 32, 32], replicated, may hold values from -0.3125 to 0.3125
- middle_first: bfloat16 [3, 3, 3, 64, 32], replicated, may hold values from -0.3125 to 0.3125
- middle_second: bfloat16 [3, 3, 3, 64, 64], replicated, may hold values from -0.21875 to 0.21875
- bottom_first: bfloat16 [3, 3, 3, 256, 64], P(None, None, None, 'rows'), may hold values from -0.21875 to 0.21875
- bottom_second: bfloat16 [3, 3, 3, 256, 256], P(None, None, None, 'rows'), may hold values from -0.109375 to 0.109375
- upsample_bottom: bfloat16 [2, 2, 2, 64, 256], replicated, may hold values from -1.5 to 1.5
- middle_merge: bfloat16 [3, 3, 3, 64, 128], replicated, may hold values from -0.078125 to 0.078125
- middle_refine: bfloat16 [3, 3, 3, 64, 64], replicated, may hold values from -0.21875 to 0.21875
- upsample_middle: bfloat16 [2, 2, 2, 32, 64], replicated, may hold values from -1.5 to 1.5
- fine_merge: bfloat16 [3, 3, 3, 32, 64], replicated, may hold values from -0.109375 to 0.109375
- fine_refine: bfloat16 [3, 3, 3, 32, 32], replicated, may hold values from -0.3125 to 0.3125
Outputs:
- decoded: bfloat16 [32, 128, 8, 512], P(None, ('groups', 'rows')), parts along dimension 1
The draws below stay inside these ranges and needn't reach their ends.
There are 2 independent parts, one for each index of `groups`. The reference program is written for one: setup_inputs(seed, part) draws one part's arguments, and reference() takes and returns one part's arrays. A program takes and returns all parts, laid end to end along the dimension named above; an argument that names none is the same for every part. Nothing has to cross between parts.
All inputs are finite; a program needn't handle non-finite values.
Results may differ from the reference program's by a relative error of at most 0.02.
Values may be sent and summed in bfloat16 or wider, within the bound.
A program may use at most 128 MiB of HBM per device.

```python
import jax
import jax.numpy as jnp
from jax import lax

C1 = 32
C2 = 64
C3 = 256
DEPTH = 8
WIDTH = 512
HEIGHT = 64


def block_levels(rng, dims, cuts, smallest, high):
    def one(axis_at, blocks):
        draws = jax.random.uniform(jax.random.fold_in(jax.random.fold_in(rng, 6), axis_at), (blocks,), jnp.float32, smallest / len(cuts), high / len(cuts))
        return jnp.repeat(jnp.exp(draws), dims[axis_at] // blocks).reshape((-1,) + (1,) * (len(dims) - axis_at - 1))

    loudness = one(*cuts[0])
    for cut in cuts[1:]:
        loudness = loudness * one(*cut)
    return loudness


def bell_draw(own_key, dims, scale, limit, split=(), held_as=jnp.bfloat16):
    array = scale * jax.random.normal(own_key, dims, jnp.float32)
    if split:
        array = array * block_levels(own_key, dims, split, -0.22, 0.18)
    return jnp.clip(array, -limit, limit).astype(held_as)


def setup_inputs(seed: int = 0, part: int = 0) -> dict:
    seeds = jax.random.split(jax.random.key(seed), 14)
    own_keys = jax.random.split(jax.random.fold_in(seeds[13], part), 14)
    volume = bell_draw(own_keys[0], (C1, HEIGHT, DEPTH, WIDTH), 1.0, 6.0, ((1, 16),))
    fine_first = bell_draw(seeds[1], (3, 3, 3, C1, C1), (27 * C1 // 2) ** -0.5, 0.3125)
    fine_second = bell_draw(seeds[2], (3, 3, 3, C1, C1), (27 * C1 // 2) ** -0.5, 0.3125)
    middle_first = bell_draw(seeds[3], (3, 3, 3, C2, C1), (27 * C1 // 2) ** -0.5, 0.3125)
    middle_second = bell_draw(seeds[4], (3, 3, 3, C2, C2), (27 * C2 // 2) ** -0.5, 0.21875)
    bottom_first = bell_draw(seeds[5], (3, 3, 3, C3, C2), (27 * C2 // 2) ** -0.5, 0.21875, ((3, 16),))
    bottom_second = bell_draw(seeds[6], (3, 3, 3, C3, C3), (27 * C3 // 2) ** -0.5, 0.109375, ((3, 16),))
    upsample_bottom = bell_draw(seeds[7], (2, 2, 2, C2, C3), (C3 // 16) ** -0.5, 1.5)
    middle_merge = bell_draw(seeds[8], (3, 3, 3, C2, 2 * C2), (108 * C2) ** -0.5, 0.078125)
    middle_refine = bell_draw(seeds[9], (3, 3, 3, C2, C2), (27 * C2 // 2) ** -0.5, 0.21875)
    upsample_middle = bell_draw(seeds[10], (2, 2, 2, C1, C2), (C2 // 4) ** -0.5, 1.5)
    fine_merge = bell_draw(seeds[11], (3, 3, 3, C1, 2 * C1), (108 * C1) ** -0.5, 0.109375)
    fine_refine = bell_draw(seeds[12], (3, 3, 3, C1, C1), (27 * C1 // 2) ** -0.5, 0.3125)
    return {"volume": volume, "fine_first": fine_first, "fine_second": fine_second, "middle_first": middle_first, "middle_second": middle_second, "bottom_first": bottom_first, "bottom_second": bottom_second, "upsample_bottom": upsample_bottom, "middle_merge": middle_merge, "middle_refine": middle_refine, "upsample_middle": upsample_middle, "fine_merge": fine_merge, "fine_refine": fine_refine}


leakage = 0.01


def conv_layer(features, kernel):
    result = lax.conv_general_dilated(features[None].astype(jnp.float32), kernel.astype(jnp.float32), (1, 1, 1), ((1, 1), (1, 1), (1, 1)), dimension_numbers=("NCDHW", "DHWOI", "NCDHW"), precision=lax.Precision.HIGHEST)
    return jax.nn.leaky_relu(result[0], leakage).astype(jnp.bfloat16)


def max_pool(features):
    chans, height, depth, width = features.shape
    return features.reshape(chans, height // 2, 2, depth // 2, 2, width // 2, 2).max(axis=(2, 4, 6))


def up_sample(features, kernel):
    chans, height, depth, width = features.shape
    result = jnp.einsum("abcoi,ihzw->ohazbwc", kernel.astype(jnp.float32), features.astype(jnp.float32), precision=lax.Precision.HIGHEST)
    return result.reshape(kernel.shape[3], 2 * height, 2 * depth, 2 * width).astype(jnp.bfloat16)


def reference(volume, fine_first, fine_second, middle_first, middle_second, bottom_first, bottom_second, upsample_bottom, middle_merge, middle_refine, upsample_middle, fine_merge, fine_refine):
    fine_one = conv_layer(volume, fine_first)
    fine_two = conv_layer(fine_one, fine_second)
    middle_one = conv_layer(max_pool(fine_two), middle_first)
    middle_two = conv_layer(middle_one, middle_second)
    bottom_one = conv_layer(max_pool(middle_two), bottom_first)
    bottom_two = conv_layer(bottom_one, bottom_second)
    lifted = up_sample(bottom_two, upsample_bottom)
    middle_three = conv_layer(jnp.concatenate([middle_two, lifted], axis=0), middle_merge)
    middle_four = conv_layer(middle_three, middle_refine)
    raised = up_sample(middle_four, upsample_middle)
    fine_three = conv_layer(jnp.concatenate([fine_two, raised], axis=0), fine_merge)
    return conv_layer(fine_three, fine_refine)
```

```python
import functools

import jax
import jax.numpy as jnp
from jax import lax
from jax.experimental import pallas as pl
from jax.experimental.pallas import tpu as pltpu
from jax.sharding import PartitionSpec as P

leakage = 0.01
bf16, f32 = jnp.bfloat16, jnp.float32
VMEM_LIMIT = 56 * 2**20


def iota(shape, axis):
    return lax.broadcasted_iota(jnp.int32, shape, axis)


def one_hot(mask):
    return jnp.where(mask, 1.0, 0.0).astype(bf16)


def dot(a, b):
    return jnp.dot(a, b, preferred_element_type=f32)


def spread(total, channels, offset, copies):
    shape = (total, copies * channels)
    return one_hot((iota(shape, 1) & (channels - 1)) + offset == iota(shape, 0))


def band(target, tap, outs, ins, depth):
    block = iota((outs, depth * ins), 1) // ins
    zero = jnp.zeros((outs, depth * ins), f32)
    for a in range(3):
        for c in range(3):
            taps = [tap(a, b, c) for b in range(3)]
            for z in range(depth):
                rows = zero
                for b in range(3):
                    if 0 <= z + b - 1 < depth:
                        rows = jnp.where(block == z + b - 1, taps[b], rows)
                start = (c * depth + z) * outs
                target[start : start + outs, a * depth * ins : (a + 1) * depth * ins] = rows.astype(bf16)


def band_kernel(target, kernel_ref, outs, total, ins, offset, depth):
    picks = spread(total, ins, offset, depth)

    def tap(a, b, c):
        at = ((a * 3 + b) * 3 + c) * outs
        return dot(kernel_ref[at : at + outs, :], picks)

    band(target, tap, outs, ins, depth)


def finish(sums, count):
    width = sums.shape[1]
    lane = iota((count, width), 1)
    left = jnp.where(lane == 0, 0.0, pltpu.roll(sums[:count], 1, 1))
    right = jnp.where(lane == width - 1, 0.0, pltpu.roll(sums[2 * count :], width - 1, 1))
    total = left + sums[count : 2 * count] + right
    return jnp.maximum(total, leakage * total).astype(bf16)


def conv_rows(sources, store, height, count, arrive):
    def row(at):
        sums = None
        for banded, rows, cells in sources:
            part = dot(banded[...], rows[pl.ds(pl.multiple_of(at * cells, cells), 3 * cells), :])
            sums = part if sums is None else sums + part
        store(at, finish(sums, count))

    if height > 2:

        @pl.loop(1, height - 1)
        def _(at):
            row(at)

    arrive()
    if height == 1:
        row(0)
    else:

        @pl.loop(0, 2)
        def _(end):
            row(end * (height - 1))


class Edges:
    def __init__(self, groups, rows, count, send, recv):
        self.group, self.me, self.count = lax.axis_index(groups), lax.axis_index(rows), count
        self.send, self.recv = send, recv

    def greet(self):
        barrier = pltpu.get_barrier_semaphore()

        @pl.when(self.me > 0)
        def _():
            pl.semaphore_signal(barrier, inc=1, device_id=(self.group, self.me - 1), device_id_type=pl.DeviceIdType.MESH)

        @pl.when(self.me < self.count - 1)
        def _():
            pl.semaphore_signal(barrier, inc=1, device_id=(self.group, self.me + 1), device_id_type=pl.DeviceIdType.MESH)

        inner = (self.me > 0) & (self.me < self.count - 1)

        @pl.when(inner)
        def _():
            pl.semaphore_wait(barrier, 2)

        @pl.when(jnp.logical_not(inner))
        def _():
            pl.semaphore_wait(barrier, 1)

    def copies(self, buf, height, cells, at):
        def one(source, target, way, step):
            return pltpu.make_async_remote_copy(
                src_ref=buf.at[pl.ds(source * cells, cells)],
                dst_ref=buf.at[pl.ds(target * cells, cells)],
                send_sem=self.send.at[at, way],
                recv_sem=self.recv.at[at, way],
                device_id=(self.group, self.me + step),
                device_id_type=pl.DeviceIdType.MESH,
            )

        return one(1, height + 1, 0, -1), one(height, 0, 1, 1)

    def start(self, buf, height, cells, at):
        up, down = self.copies(buf, height, cells, at)

        @pl.when(self.me > 0)
        def _():
            up.start()

        @pl.when(self.me < self.count - 1)
        def _():
            down.start()

    def arrive(self, buf, height, cells, at):
        up, down = self.copies(buf, height, cells, at)
        zero = jnp.zeros((cells, buf.shape[1]), bf16)

        @pl.when(self.me < self.count - 1)
        def _():
            up.wait_recv()

        @pl.when(self.me == self.count - 1)
        def _():
            buf[(height + 1) * cells : (height + 2) * cells, :] = zero

        @pl.when(self.me > 0)
        def _():
            down.wait_recv()

        @pl.when(self.me == 0)
        def _():
            buf[0:cells, :] = zero

    def sent(self, buf, height, cells, at):
        up, down = self.copies(buf, height, cells, at)

        @pl.when(self.me > 0)
        def _():
            up.wait_send()

        @pl.when(self.me < self.count - 1)
        def _():
            down.wait_send()


def into(buf, cells):
    def store(at, value):
        buf[pl.ds(pl.multiple_of((at + 1) * cells, cells), cells), :] = value

    return store


def plain(buf, cells):
    def store(at, value):
        buf[pl.ds(pl.multiple_of(at * cells, cells), cells), :] = value

    return store


def halves(width):
    half = width // 2
    source, target = iota((width, width), 0), iota((width, width), 1)
    return one_hot(source == jnp.where(target < half, 2 * target, 2 * (target - half) + 1))


def weave(width):
    half = width // 2
    source, target = iota((width, width), 0), iota((width, width), 1)
    return one_hot(target == jnp.where(source < half, 2 * source, 2 * (source - half) + 1))


def pool(first, second, chans, parts):
    rows = jnp.maximum(first, second)
    depth, width = rows.shape[0] // chans, rows.shape[1]
    pairs = [
        jnp.maximum(rows[z * chans : (z + 1) * chans], rows[(z + 1) * chans : (z + 2) * chans])
        for z in range(0, depth, 2)
    ]
    split = dot(jnp.concatenate(pairs, axis=0), parts)
    return jnp.maximum(split[:, : width // 2], split[:, width // 2 :]).astype(bf16)


def lift(rows, kernel_ref, ins, outs, woven, store):
    depth = rows.shape[0] // ins
    parts = [dot(kernel_ref[...], rows[z * ins : (z + 1) * ins]).astype(bf16) for z in range(depth)]
    for a in range(2):
        stack = []
        for z in range(depth):
            for b in range(2):
                at = (a * 2 + b) * 2 * outs
                stack.append(jnp.concatenate([parts[z][at : at + outs], parts[z][at + outs : at + 2 * outs]], axis=1))
        store(a, dot(jnp.concatenate(stack, axis=0), woven).astype(bf16))


def encoder(size, groups, rows, count, *refs):
    (vol, k1, k2, k3, k4, fine_out, mid_out, low_out) = refs[:8]
    (b_vol, b_one, b_pool, b_mid, t1, t2, t3, t4, send, recv, local) = refs[8:]
    H, Z, W, C1, C2 = size
    R, R2, RP = Z * C1, Z // 2 * C2, Z // 2 * C1
    edges = Edges(groups, rows, count, send, recv)
    load = pltpu.make_async_copy(vol, b_vol.at[pl.ds(R, H * R)], local)
    load.start()
    edges.greet()
    load.wait()
    edges.start(b_vol, H, R, 0)
    band_kernel(t1, k1, C1, C1, C1, 0, Z)
    conv_rows([(t1, b_vol, R)], into(b_one, R), H, R, lambda: edges.arrive(b_vol, H, R, 0))
    edges.start(b_one, H, R, 1)
    band_kernel(t2, k2, C1, C1, C1, 0, Z)
    conv_rows([(t2, b_one, R)], plain(fine_out, R), H, R, lambda: edges.arrive(b_one, H, R, 1))
    parts = halves(W)
    for h in range(H // 2):
        first, second = fine_out[2 * h * R : (2 * h + 1) * R, :], fine_out[(2 * h + 1) * R : (2 * h + 2) * R, :]
        b_pool[(h + 1) * RP : (h + 2) * RP, :] = pool(first, second, C1, parts)
    edges.start(b_pool, H // 2, RP, 2)
    band_kernel(t3, k3, C2, C1, C1, 0, Z // 2)
    conv_rows([(t3, b_pool, RP)], into(b_mid, R2), H // 2, R2, lambda: edges.arrive(b_pool, H // 2, RP, 2))
    edges.start(b_mid, H // 2, R2, 3)
    band_kernel(t4, k4, C2, C2, C2, 0, Z // 2)
    conv_rows([(t4, b_mid, R2)], plain(mid_out, R2), H // 2, R2, lambda: edges.arrive(b_mid, H // 2, R2, 3))
    parts = halves(W // 2)
    R3 = R2 // 2
    for h in range(H // 4):
        first, second = mid_out[2 * h * R2 : (2 * h + 1) * R2, :], mid_out[(2 * h + 1) * R2 : (2 * h + 2) * R2, :]
        low_out[h * R3 : (h + 1) * R3, :] = pool(first, second, C2, parts)
    edges.sent(b_vol, H, R, 0)
    edges.sent(b_one, H, R, 1)
    edges.sent(b_pool, H // 2, RP, 2)
    edges.sent(b_mid, H // 2, R2, 3)


def decoder(size, groups, rows, count, *refs):
    (fine, mid, low, whole, ub, mm, mr, um, fm, fr, out) = refs[:11]
    (b_fine, b_mid, b_low, b_bot, bot, b_lift, b_three, four, b_raise, b_last) = refs[11:21]
    (kt, t1, t2, t3a, t3b, t4, t5a, t5b, t6, send, recv, local) = refs[21:]
    H, Z, W, C1, C2, C3 = size
    R, R2, RP, RB = Z * C1, Z // 2 * C2, Z // 4 * C2, Z // 4 * C3
    H2, H4 = H // 2, H // 4
    edges = Edges(groups, rows, count, send, recv)
    loads = [
        pltpu.make_async_copy(low, b_low.at[pl.ds(RP, H4 * RP)], local.at[0]),
        pltpu.make_async_copy(mid, b_mid.at[pl.ds(R2, H2 * R2)], local.at[1]),
        pltpu.make_async_copy(fine, b_fine.at[pl.ds(R, H * R)], local.at[2]),
    ]
    for load in loads:
        load.start()
    edges.greet()
    loads[0].wait()
    edges.start(b_low, H4, RP, 0)
    loads[1].wait()
    edges.start(b_mid, H2, R2, 1)
    loads[2].wait()
    edges.start(b_fine, H, R, 2)
    side = C3 // C2
    each = -(-27 // side)
    wide = Z // 4 * C2
    shape = (C3, side * wide)
    picks = one_hot(iota(shape, 0) == iota(shape, 1) // wide * C2 + (iota(shape, 1) & (C2 - 1)))
    for t in range(each):
        taps = dot(whole[:, 27 + t].reshape(C3, C3), picks).astype(bf16)
        for q in range(side):
            if q * each + t < 27:
                at = (q * each + t) * C3
                kt[at : at + C3, :] = taps[:, q * wide : (q + 1) * wide]

    def tap(a, b, c):
        at = ((a * 3 + b) * 3 + c) * C3
        return kt[at : at + C3, :].astype(f32)

    band(t1, tap, C3, C2, Z // 4)
    conv_rows([(t1, b_low, RP)], into(b_bot, RB), H4, RB, lambda: edges.arrive(b_low, H4, RP, 0))
    edges.start(b_bot, H4, RB, 3)
    for a in range(3):
        for c in range(3):
            for z in range(Z // 4):
                for y in range(Z // 4):
                    r, l = (c * (Z // 4) + z) * C3, (a * (Z // 4) + y) * C3
                    if -1 <= y - z <= 1:
                        t2[r : r + C3, l : l + C3] = whole[:, (a * 3 + y - z + 1) * 3 + c].reshape(C3, C3)
                    else:
                        t2[r : r + C3, l : l + C3] = jnp.zeros((C3, C3), bf16)
    conv_rows([(t2, b_bot, RB)], plain(bot, RB), H4, RB, lambda: edges.arrive(b_bot, H4, RB, 3))
    woven = weave(W // 2)
    for h in range(H4):

        def store(a, value):
            at = (2 * h + a + 1) * R2
            b_lift[at : at + R2, :] = value

        lift(bot[h * RB : (h + 1) * RB, :], ub, C3, C2, woven, store)
    edges.start(b_lift, H2, R2, 4)
    band_kernel(t3a, mm, C2, 2 * C2, C2, 0, Z // 2)
    band_kernel(t3b, mm, C2, 2 * C2, C2, C2, Z // 2)

    def both():
        edges.arrive(b_mid, H2, R2, 1)
        edges.arrive(b_lift, H2, R2, 4)

    conv_rows([(t3a, b_mid, R2), (t3b, b_lift, R2)], into(b_three, R2), H2, R2, both)
    edges.start(b_three, H2, R2, 5)
    band_kernel(t4, mr, C2, C2, C2, 0, Z // 2)
    conv_rows([(t4, b_three, R2)], plain(four, R2), H2, R2, lambda: edges.arrive(b_three, H2, R2, 5))
    woven = weave(W)
    for h in range(H2):

        def store(a, value):
            at = (2 * h + a + 1) * R
            b_raise[at : at + R, :] = value

        lift(four[h * R2 : (h + 1) * R2, :], um, C2, C1, woven, store)
    edges.start(b_raise, H, R, 6)
    band_kernel(t5a, fm, C1, 2 * C1, C1, 0, Z)
    band_kernel(t5b, fm, C1, 2 * C1, C1, C1, Z)

    def last():
        edges.arrive(b_fine, H, R, 2)
        edges.arrive(b_raise, H, R, 6)

    conv_rows([(t5a, b_fine, R), (t5b, b_raise, R)], into(b_last, R), H, R, last)
    edges.start(b_last, H, R, 7)
    band_kernel(t6, fr, C1, C1, C1, 0, Z)
    conv_rows([(t6, b_last, R)], plain(out, R), H, R, lambda: edges.arrive(b_last, H, R, 7))
    for at, (buf, height, cells) in enumerate(
        [(b_low, H4, RP), (b_mid, H2, R2), (b_fine, H, R), (b_bot, H4, RB), (b_lift, H2, R2), (b_three, H2, R2), (b_raise, H, R), (b_last, H, R)]
    ):
        edges.sent(buf, height, cells, at)


def per_device(count, *args):
    (volume, f1, f2, m1, m2, b1, b2, ub, mm, mr, um, fm, fr) = args
    C1, H, Z, W = volume.shape
    C2, C3 = m1.shape[3], b2.shape[4]
    own = b1.shape[3]
    R, R2, RP, RL, RB = Z * C1, Z // 2 * C2, Z // 2 * C1, Z // 4 * C2, Z // 4 * C3
    H2, H4, W2, W4 = H // 2, H // 4, W // 2, W // 4
    flat = lambda k: k.reshape(-1, k.shape[-1])
    side = C3 // C2
    each = -(-27 // side)
    first = jnp.pad(b1.reshape(27, own, C2), ((0, each * side - 27), (0, 0), (0, 0))).reshape(side, each, own, C2)
    first = jnp.concatenate([first[q] for q in range(side)], axis=-1)
    packed = jnp.concatenate([b2.reshape(27, own, C3), first], axis=0)
    whole = lax.all_gather(packed, "rows", axis=0)
    cells = volume.transpose(1, 2, 0, 3).reshape(H * R, W)
    vmem, hbm = pl.BlockSpec(memory_space=pltpu.VMEM), pl.BlockSpec(memory_space=pl.ANY)
    V = lambda r, c: pltpu.VMEM((r, c), bf16)
    D = pltpu.SemaphoreType.DMA
    fine, mid, low = pl.pallas_call(
        functools.partial(encoder, (H, Z, W, C1, C2), "groups", "rows", count),
        out_shape=[jax.ShapeDtypeStruct(s, bf16) for s in ((H * R, W), (H2 * R2, W2), (H4 * RL, W4))],
        in_specs=[hbm] + [vmem] * 4,
        out_specs=[vmem] * 3,
        scratch_shapes=[
            V((H + 2) * R, W), V((H + 2) * R, W), V((H2 + 2) * RP, W2), V((H2 + 2) * R2, W2),
            V(3 * R, 3 * R), V(3 * R, 3 * R), V(3 * R2, 3 * RP), V(3 * R2, 3 * R2),
            D((4, 2)), D((4, 2)), D,
        ],
        compiler_params=pltpu.CompilerParams(collective_id=0, has_side_effects=True, vmem_limit_bytes=VMEM_LIMIT),
        cost_estimate=pl.CostEstimate(flops=10**10, bytes_accessed=10**8, transcendentals=0),
        name="encoder",
    )(cells, flat(f1), flat(f2), flat(m1), flat(m2))
    out = pl.pallas_call(
        functools.partial(decoder, (H, Z, W, C1, C2, C3), "groups", "rows", count),
        out_shape=jax.ShapeDtypeStruct((H * R, W), bf16),
        in_specs=[hbm] * 3 + [vmem] * 7,
        out_specs=vmem,
        scratch_shapes=[
            V((H + 2) * R, W), V((H2 + 2) * R2, W2), V((H4 + 2) * RL, W4), V((H4 + 2) * RB, W4), V(H4 * RB, W4),
            V((H2 + 2) * R2, W2), V((H2 + 2) * R2, W2), V(H2 * R2, W2), V((H + 2) * R, W), V((H + 2) * R, W),
            V(27 * C3, Z // 4 * C2), V(3 * RB, 3 * RL), V(3 * RB, 3 * RB), V(3 * R2, 3 * R2), V(3 * R2, 3 * R2),
            V(3 * R2, 3 * R2), V(3 * R, 3 * R), V(3 * R, 3 * R), V(3 * R, 3 * R),
            D((8, 2)), D((8, 2)), D((3,)),
        ],
        compiler_params=pltpu.CompilerParams(collective_id=1, has_side_effects=True, vmem_limit_bytes=VMEM_LIMIT),
        cost_estimate=pl.CostEstimate(flops=10**10, bytes_accessed=10**8, transcendentals=0),
        name="decoder",
    )(fine, mid, low, whole, flat(ub), flat(mm), flat(mr), flat(um), flat(fm), flat(fr))
    return out.reshape(H, Z, C1, W).transpose(2, 0, 1, 3)


def solution(mesh):
    placed = [P(None, ("groups", "rows"), None, None)] + [P()] * 12
    placed[5] = placed[6] = P(None, None, None, "rows", None)
    return jax.shard_map(
        functools.partial(per_device, mesh.shape["rows"]),
        mesh=mesh,
        in_specs=tuple(placed),
        out_specs=P(None, ("groups", "rows"), None, None),
        check_vma=False,
    )
```

```python
import functools

import jax
import jax.numpy as jnp
from jax import lax
from jax.experimental import pallas as pl
from jax.experimental.pallas import tpu as pltpu
from jax.sharding import PartitionSpec as P

leakage = 0.01
bf16, f32 = jnp.bfloat16, jnp.float32
VMEM_LIMIT = 56 * 2**20


def iota(shape, axis):
    return lax.broadcasted_iota(jnp.int32, shape, axis)


def one_hot(mask):
    return jnp.where(mask, 1.0, 0.0).astype(bf16)


def dot(a, b):
    return jnp.dot(a, b, preferred_element_type=f32)


def spread(total, channels, offset, copies):
    shape = (total, copies * channels)
    return one_hot((iota(shape, 1) & (channels - 1)) + offset == iota(shape, 0))


def band(target, tap, outs, ins, depth):
    block = iota((outs, depth * ins), 1) // ins
    zero = jnp.zeros((outs, depth * ins), f32)
    for a in range(3):
        for c in range(3):
            taps = [tap(a, b, c) for b in range(3)]
            for z in range(depth):
                rows = zero
                for b in range(3):
                    if 0 <= z + b - 1 < depth:
                        rows = jnp.where(block == z + b - 1, taps[b], rows)
                start = (c * depth + z) * outs
                target[start : start + outs, a * depth * ins : (a + 1) * depth * ins] = rows.astype(bf16)


def band_kernel(target, kernel_ref, outs, total, ins, offset, depth, turned=False):
    picks = spread(total, ins, offset, depth)

    def tap(a, b, c):
        at = (a * 3 + b) * 3 + c
        if turned:
            block = kernel_ref[at * total : (at + 1) * total, :]
            return lax.dot_general(block, picks, (((0,), (0,)), ((), ())), preferred_element_type=f32)
        return dot(kernel_ref[at * outs : (at + 1) * outs, :], picks)

    band(target, tap, outs, ins, depth)


def finish(sums, count):
    width = sums.shape[1]
    lane = iota((count, width), 1)
    left = jnp.where(lane == 0, 0.0, pltpu.roll(sums[:count], 1, 1))
    right = jnp.where(lane == width - 1, 0.0, pltpu.roll(sums[2 * count :], width - 1, 1))
    total = left + sums[count : 2 * count] + right
    return jnp.maximum(total, leakage * total).astype(bf16)


def conv_rows(sources, store, height, count, arrive, before=lambda: None):
    def row(at):
        sums = None
        for banded, rows, cells in sources:
            part = dot(banded[...], rows[pl.ds(pl.multiple_of(at * cells, cells), 3 * cells), :])
            sums = part if sums is None else sums + part
        store(at, finish(sums, count))

    if height > 2:

        @pl.loop(1, height - 1)
        def _(at):
            row(at)

    before()
    arrive()
    if height == 1:
        row(0)
    else:

        @pl.loop(0, 2)
        def _(end):
            row(end * (height - 1))


class Edges:
    def __init__(self, groups, rows, count, send, recv):
        self.group, self.me, self.count = lax.axis_index(groups), lax.axis_index(rows), count
        self.send, self.recv = send, recv

    def greet(self, others):
        barrier = pltpu.get_barrier_semaphore()

        def signal(to):
            pl.semaphore_signal(barrier, inc=1, device_id=(self.group, to), device_id_type=pl.DeviceIdType.MESH)

        for other in others:
            signal(other)

        @pl.when(self.me > 0)
        def _():
            signal(self.me - 1)

        @pl.when(self.me < self.count - 1)
        def _():
            signal(self.me + 1)

        inner = (self.me > 0) & (self.me < self.count - 1)

        @pl.when(inner)
        def _():
            pl.semaphore_wait(barrier, 2 + len(others))

        @pl.when(jnp.logical_not(inner))
        def _():
            pl.semaphore_wait(barrier, 1 + len(others))

    def copies(self, buf, height, cells, at):
        def one(source, target, way, step):
            return pltpu.make_async_remote_copy(
                src_ref=buf.at[pl.ds(source * cells, cells)],
                dst_ref=buf.at[pl.ds(target * cells, cells)],
                send_sem=self.send.at[at, way],
                recv_sem=self.recv.at[at, way],
                device_id=(self.group, self.me + step),
                device_id_type=pl.DeviceIdType.MESH,
            )

        return one(1, height + 1, 0, -1), one(height, 0, 1, 1)

    def start(self, buf, height, cells, at):
        up, down = self.copies(buf, height, cells, at)

        @pl.when(self.me > 0)
        def _():
            up.start()

        @pl.when(self.me < self.count - 1)
        def _():
            down.start()

    def arrive(self, buf, height, cells, at):
        up, down = self.copies(buf, height, cells, at)
        zero = jnp.zeros((cells, buf.shape[1]), bf16)

        @pl.when(self.me < self.count - 1)
        def _():
            up.wait_recv()

        @pl.when(self.me == self.count - 1)
        def _():
            buf[(height + 1) * cells : (height + 2) * cells, :] = zero

        @pl.when(self.me > 0)
        def _():
            down.wait_recv()

        @pl.when(self.me == 0)
        def _():
            buf[0:cells, :] = zero

    def sent(self, buf, height, cells, at):
        up, down = self.copies(buf, height, cells, at)

        @pl.when(self.me > 0)
        def _():
            up.wait_send()

        @pl.when(self.me < self.count - 1)
        def _():
            down.wait_send()


class Ring:
    def __init__(self, edges, whole, send, recv, side_send, side_recv):
        self.edges, self.whole = edges, whole
        self.sems = send, recv, side_send, side_recv
        self.chips = edges.count // 2
        self.core = lax.rem(edges.me, 2)
        chip = edges.me // 2
        self.place = jnp.where(lax.rem(chip, 2) == 0, chip // 2, self.chips - 1 - chip // 2)
        self.mate = edges.me + 1 - 2 * self.core
        self.cut = whole.shape[1] // 2

    def at(self, place):
        place = lax.rem(place + 2 * self.chips, self.chips)
        chip = jnp.where(place < self.chips // 2, 2 * place, 2 * (self.chips - 1 - place) + 1)
        return 2 * chip + self.core

    def neighbours(self):
        return [self.at(self.place + 1), self.at(self.place - 1)]

    def copy(self, slot, way, to, send, recv):
        part = self.whole.at[slot, pl.ds(way * self.cut, self.cut)]
        return pltpu.make_async_remote_copy(
            src_ref=part,
            dst_ref=part,
            send_sem=send,
            recv_sem=recv,
            device_id=(self.edges.group, to),
            device_id_type=pl.DeviceIdType.MESH,
        )

    def hop(self, step, way):
        sign = 1 - 2 * way
        send, recv = self.sems[0].at[step, way], self.sems[1].at[step, way]
        return self.copy(self.at(self.place - sign * step), way, self.at(self.place + sign), send, recv)

    def landed(self, step, way):
        sign = 1 - 2 * way
        send, recv = self.sems[0].at[step, way], self.sems[1].at[step, way]
        return self.copy(self.at(self.place - sign * (step + 1)), way, self.at(self.place + sign), send, recv)

    def across(self, step, way, other=False):
        sign = 1 - 2 * way
        slot = self.at(self.place - sign * (step + 1))
        slot = slot + 1 - 2 * self.core if other else slot
        return self.copy(slot, way, self.mate, self.sems[2].at[step + 1, way], self.sems[3].at[step + 1, way])

    def step(self, at):
        if isinstance(at, int) and at >= self.chips:
            return
        for way in range(2):
            if not isinstance(at, int) or at > 0:
                self.landed(at - 1, way).wait_recv()
            if not isinstance(at, int) or at < self.chips - 1:
                self.hop(at, way).start()
            self.across(at - 1, way).start()

    def finish(self, done):
        if done < self.chips:

            @pl.loop(done, self.chips - 1)
            def _(at):
                self.step(at)

            self.step(self.chips - 1)

        @pl.loop(0, self.chips)
        def _(at):
            for way in range(2):
                self.across(at - 1, way, True).wait_recv()

    def sent(self):
        @pl.loop(0, self.chips)
        def _(at):
            for way in range(2):
                self.across(at - 1, way).wait_send()

        @pl.loop(0, self.chips - 1)
        def _(at):
            for way in range(2):
                self.hop(at, way).wait_send()


def into(buf, cells):
    def store(at, value):
        buf[pl.ds(pl.multiple_of((at + 1) * cells, cells), cells), :] = value

    return store


def plain(buf, cells):
    def store(at, value):
        buf[pl.ds(pl.multiple_of(at * cells, cells), cells), :] = value

    return store


def halves(width):
    half = width // 2
    source, target = iota((width, width), 0), iota((width, width), 1)
    return one_hot(source == jnp.where(target < half, 2 * target, 2 * (target - half) + 1))


def weave(width):
    half = width // 2
    source, target = iota((width, width), 0), iota((width, width), 1)
    return one_hot(target == jnp.where(source < half, 2 * source, 2 * (source - half) + 1))


def pool(first, second, chans, parts):
    rows = jnp.maximum(first, second)
    depth, width = rows.shape[0] // chans, rows.shape[1]
    pairs = [
        jnp.maximum(rows[z * chans : (z + 1) * chans], rows[(z + 1) * chans : (z + 2) * chans])
        for z in range(0, depth, 2)
    ]
    split = dot(jnp.concatenate(pairs, axis=0), parts)
    return jnp.maximum(split[:, : width // 2], split[:, width // 2 :]).astype(bf16)


def lift(rows, kernel_ref, ins, outs, woven, store):
    depth = rows.shape[0] // ins
    parts = [dot(kernel_ref[...], rows[z * ins : (z + 1) * ins]).astype(bf16) for z in range(depth)]
    for a in range(2):
        stack = []
        for z in range(depth):
            for b in range(2):
                at = (a * 2 + b) * 2 * outs
                stack.append(jnp.concatenate([parts[z][at : at + outs], parts[z][at + outs : at + 2 * outs]], axis=1))
        store(a, dot(jnp.concatenate(stack, axis=0), woven).astype(bf16))


def network(size, groups, rows, count, *refs):
    (vol, b2, b1, k1, k2, k3, k4, ub, mm, mr, um, fm, fr, out) = refs[:14]
    (b_vol, b_one, b_pool, b_first, e1, e2, e3, e4) = refs[14:22]
    (b_fine, b_mid, b_low, b_bot, bot, b_lift, b_three, four, b_raise, b_last) = refs[22:32]
    (kt, t1, t2, t3a, t3b, t4, t5a, t5b, t6, whole) = refs[32:42]
    (send, recv, ring_send, ring_recv, side_send, side_recv, local) = refs[42:]
    H, Z, W, C1, C2, C3 = size
    R, R2, RP, RB = Z * C1, Z // 2 * C2, Z // 4 * C2, Z // 4 * C3
    RQ = Z // 2 * C1
    H2, H4 = H // 2, H // 4
    side = C3 // C2
    each = -(-27 // side)
    edges = Edges(groups, rows, count, send, recv)
    ring = Ring(edges, whole, ring_send, ring_recv, side_send, side_recv)
    loads = [
        pltpu.make_async_copy(vol, b_vol.at[pl.ds(R, H * R)], local.at[0]),
        pltpu.make_async_copy(b2, whole.at[edges.me, pl.ds(0, 27)], local.at[1]),
    ]
    for load in loads:
        load.start()
    for t in range(each):
        taps = [b1[q * each + t] if q * each + t < 27 else jnp.zeros(b1.shape[1:], bf16) for q in range(side)]
        whole[edges.me, 27 + t] = jnp.concatenate(taps, axis=-1)
    edges.greet(ring.neighbours())
    loads[0].wait()
    edges.start(b_vol, H, R, 8)
    loads[1].wait()
    ring.step(0)
    band_kernel(e1, k1, C1, C1, C1, 0, Z)
    conv_rows([(e1, b_vol, R)], into(b_one, R), H, R, lambda: edges.arrive(b_vol, H, R, 8), lambda: ring.step(1))
    edges.start(b_one, H, R, 9)
    ring.step(2)
    band_kernel(e2, k2, C1, C1, C1, 0, Z)
    conv_rows([(e2, b_one, R)], into(b_fine, R), H, R, lambda: edges.arrive(b_one, H, R, 9), lambda: ring.step(3))
    parts = halves(W)
    for h in range(H2):
        first, second = b_fine[(2 * h + 1) * R : (2 * h + 2) * R, :], b_fine[(2 * h + 2) * R : (2 * h + 3) * R, :]
        b_pool[(h + 1) * RQ : (h + 2) * RQ, :] = pool(first, second, C1, parts)
    edges.start(b_pool, H2, RQ, 10)
    ring.step(4)
    band_kernel(e3, k3, C2, C1, C1, 0, Z // 2, True)
    conv_rows([(e3, b_pool, RQ)], into(b_first, R2), H2, R2, lambda: edges.arrive(b_pool, H2, RQ, 10), lambda: ring.step(5))
    edges.start(b_first, H2, R2, 11)
    ring.step(6)
    band_kernel(e4, k4, C2, C2, C2, 0, Z // 2)
    conv_rows([(e4, b_first, R2)], into(b_mid, R2), H2, R2, lambda: edges.arrive(b_first, H2, R2, 11))
    parts = halves(W // 2)
    for h in range(H4):
        first, second = b_mid[(2 * h + 1) * R2 : (2 * h + 2) * R2, :], b_mid[(2 * h + 2) * R2 : (2 * h + 3) * R2, :]
        b_low[(h + 1) * RP : (h + 2) * RP, :] = pool(first, second, C2, parts)
    edges.start(b_low, H4, RP, 0)
    ring.finish(7)
    edges.start(b_mid, H2, R2, 1)
    edges.start(b_fine, H, R, 2)
    wide = Z // 4 * C2
    shape = (C3, side * wide)
    picks = one_hot(iota(shape, 0) == iota(shape, 1) // wide * C2 + (iota(shape, 1) & (C2 - 1)))
    for t in range(each):
        taps = dot(whole[:, 27 + t].reshape(C3, C3), picks).astype(bf16)
        for q in range(side):
            if q * each + t < 27:
                at = (q * each + t) * C3
                kt[at : at + C3, :] = taps[:, q * wide : (q + 1) * wide]

    def tap(a, b, c):
        at = ((a * 3 + b) * 3 + c) * C3
        return kt[at : at + C3, :].astype(f32)

    band(t1, tap, C3, C2, Z // 4)
    conv_rows([(t1, b_low, RP)], into(b_bot, RB), H4, RB, lambda: edges.arrive(b_low, H4, RP, 0))
    edges.start(b_bot, H4, RB, 3)
    for a in range(3):
        for c in range(3):
            for z in range(Z // 4):
                for y in range(Z // 4):
                    r, l = (c * (Z // 4) + z) * C3, (a * (Z // 4) + y) * C3
                    if -1 <= y - z <= 1:
                        t2[r : r + C3, l : l + C3] = whole[:, (a * 3 + y - z + 1) * 3 + c].reshape(C3, C3)
                    else:
                        t2[r : r + C3, l : l + C3] = jnp.zeros((C3, C3), bf16)
    conv_rows([(t2, b_bot, RB)], plain(bot, RB), H4, RB, lambda: edges.arrive(b_bot, H4, RB, 3))
    woven = weave(W // 2)
    for h in range(H4):

        def store(a, value):
            at = (2 * h + a + 1) * R2
            b_lift[at : at + R2, :] = value

        lift(bot[h * RB : (h + 1) * RB, :], ub, C3, C2, woven, store)
    edges.start(b_lift, H2, R2, 4)
    band_kernel(t3a, mm, C2, 2 * C2, C2, 0, Z // 2)
    band_kernel(t3b, mm, C2, 2 * C2, C2, C2, Z // 2)

    def both():
        edges.arrive(b_mid, H2, R2, 1)
        edges.arrive(b_lift, H2, R2, 4)

    conv_rows([(t3a, b_mid, R2), (t3b, b_lift, R2)], into(b_three, R2), H2, R2, both)
    edges.start(b_three, H2, R2, 5)
    band_kernel(t4, mr, C2, C2, C2, 0, Z // 2)
    conv_rows([(t4, b_three, R2)], plain(four, R2), H2, R2, lambda: edges.arrive(b_three, H2, R2, 5))
    woven = weave(W)
    for h in range(H2):

        def store(a, value):
            at = (2 * h + a + 1) * R
            b_raise[at : at + R, :] = value

        lift(four[h * R2 : (h + 1) * R2, :], um, C2, C1, woven, store)
    edges.start(b_raise, H, R, 6)
    band_kernel(t5a, fm, C1, 2 * C1, C1, 0, Z)
    band_kernel(t5b, fm, C1, 2 * C1, C1, C1, Z)

    def last():
        edges.arrive(b_fine, H, R, 2)
        edges.arrive(b_raise, H, R, 6)

    conv_rows([(t5a, b_fine, R), (t5b, b_raise, R)], into(b_last, R), H, R, last)
    edges.start(b_last, H, R, 7)
    band_kernel(t6, fr, C1, C1, C1, 0, Z)
    conv_rows([(t6, b_last, R)], plain(out, R), H, R, lambda: edges.arrive(b_last, H, R, 7))
    for at, (buf, height, cells) in enumerate(
        [(b_low, H4, RP), (b_mid, H2, R2), (b_fine, H, R), (b_bot, H4, RB), (b_lift, H2, R2), (b_three, H2, R2), (b_raise, H, R), (b_last, H, R),
         (b_vol, H, R), (b_one, H, R), (b_pool, H2, RQ), (b_first, H2, R2)]
    ):
        edges.sent(buf, height, cells, at)
    ring.sent()


def per_device(count, *args):
    (volume, f1, f2, m1, m2, b1, b2, ub, mm, mr, um, fm, fr) = args
    C1, H, Z, W = volume.shape
    C2, C3 = m1.shape[3], b2.shape[4]
    own = b1.shape[3]
    R, R2, RP, RL, RB = Z * C1, Z // 2 * C2, Z // 2 * C1, Z // 4 * C2, Z // 4 * C3
    H2, H4, W2, W4 = H // 2, H // 4, W // 2, W // 4
    flat = lambda k: k.reshape(-1, k.shape[-1])
    each = -(-27 // (C3 // C2))
    taps = 27 + each + (27 + each) % 2
    chips = count // 2
    cells = volume.transpose(1, 2, 0, 3).reshape(H * R, W)
    vmem, hbm = pl.BlockSpec(memory_space=pltpu.VMEM), pl.BlockSpec(memory_space=pl.ANY)
    V = lambda *shape: pltpu.VMEM(shape, bf16)
    D = pltpu.SemaphoreType.DMA
    out = pl.pallas_call(
        functools.partial(network, (H, Z, W, C1, C2, C3), "groups", "rows", count),
        out_shape=jax.ShapeDtypeStruct((H * R, W), bf16),
        in_specs=[hbm] * 2 + [vmem] * 11,
        out_specs=vmem,
        scratch_shapes=[
            V((H + 2) * R, W), V((H + 2) * R, W), V((H2 + 2) * RP, W2), V((H2 + 2) * R2, W2),
            V(3 * R, 3 * R), V(3 * R, 3 * R), V(3 * R2, 3 * RP), V(3 * R2, 3 * R2),
            V((H + 2) * R, W), V((H2 + 2) * R2, W2), V((H4 + 2) * RL, W4), V((H4 + 2) * RB, W4), V(H4 * RB, W4),
            V((H2 + 2) * R2, W2), V((H2 + 2) * R2, W2), V(H2 * R2, W2), V((H + 2) * R, W), V((H + 2) * R, W),
            V(27 * C3, Z // 4 * C2), V(3 * RB, 3 * RL), V(3 * RB, 3 * RB), V(3 * R2, 3 * R2), V(3 * R2, 3 * R2),
            V(3 * R2, 3 * R2), V(3 * R, 3 * R), V(3 * R, 3 * R), V(3 * R, 3 * R), V(count, taps, own, C3),
            D((12, 2)), D((12, 2)), D((chips - 1, 2)), D((chips - 1, 2)), D((chips, 2)), D((chips, 2)), D((2,)),
        ],
        compiler_params=pltpu.CompilerParams(collective_id=0, has_side_effects=True, vmem_limit_bytes=VMEM_LIMIT),
        name="network",
    )(
        cells, b2.reshape(27, own, C3), b1.reshape(27, own, C2), flat(f1), flat(f2), flat(m1.swapaxes(3, 4)), flat(m2),
        flat(ub), flat(mm), flat(mr), flat(um), flat(fm), flat(fr),
    )
    return out.reshape(H, Z, C1, W).transpose(2, 0, 1, 3)


def solution(mesh):
    placed = [P(None, ("groups", "rows"), None, None)] + [P()] * 12
    placed[5] = placed[6] = P(None, None, None, "rows", None)
    return jax.shard_map(
        functools.partial(per_device, mesh.shape["rows"]),
        mesh=mesh,
        in_specs=tuple(placed),
        out_specs=P(None, ("groups", "rows"), None, None),
        check_vma=False,
    )
```

```python
import functools

import jax
import jax.numpy as jnp
from jax import lax
from jax.experimental import pallas as pl
from jax.experimental.pallas import tpu as pltpu
from jax.sharding import PartitionSpec as P

leakage = 0.01
bf16, f32 = jnp.bfloat16, jnp.float32
VMEM_LIMIT = 56 * 2**20


def iota(shape, axis):
    return lax.broadcasted_iota(jnp.int32, shape, axis)


def one_hot(mask):
    return jnp.where(mask, 1.0, 0.0).astype(bf16)


def dot(a, b):
    return jnp.dot(a, b, preferred_element_type=f32)


def spread(total, channels, offset, copies):
    shape = (total, copies * channels)
    return one_hot((iota(shape, 1) & (channels - 1)) + offset == iota(shape, 0))


def band(target, tap, outs, ins, depth):
    block = iota((outs, depth * ins), 1) // ins
    zero = jnp.zeros((outs, depth * ins), f32)
    for a in range(3):
        for c in range(3):
            taps = [tap(a, b, c) for b in range(3)]
            for z in range(depth):
                rows = zero
                for b in range(3):
                    if 0 <= z + b - 1 < depth:
                        rows = jnp.where(block == z + b - 1, taps[b], rows)
                start = (c * depth + z) * outs
                target[start : start + outs, a * depth * ins : (a + 1) * depth * ins] = rows.astype(bf16)


def band_kernel(target, kernel_ref, outs, total, ins, offset, depth, turned=False):
    picks = spread(total, ins, offset, depth)

    def tap(a, b, c):
        at = (a * 3 + b) * 3 + c
        if turned:
            block = kernel_ref[at * total : (at + 1) * total, :]
            return lax.dot_general(block, picks, (((0,), (0,)), ((), ())), preferred_element_type=f32)
        return dot(kernel_ref[at * outs : (at + 1) * outs, :], picks)

    band(target, tap, outs, ins, depth)


def finish(sums, count):
    width = sums.shape[1]
    lane = iota((count, width), 1)
    left = jnp.where(lane == 0, 0.0, pltpu.roll(sums[:count], 1, 1))
    right = jnp.where(lane == width - 1, 0.0, pltpu.roll(sums[2 * count :], width - 1, 1))
    return left + sums[count : 2 * count] + right


def leaky(total):
    return jnp.maximum(total, leakage * total).astype(bf16)


def conv_rows(sources, store, height, count, arrive, before=lambda: None, held=None, last=leaky):
    def row(at):
        sums = None
        for banded, rows, cells in sources:
            part = dot(banded[...], rows[pl.ds(pl.multiple_of(at * cells, cells), 3 * cells), :])
            sums = part if sums is None else sums + part
        total = finish(sums, count)
        if held is not None:
            total = total + held[pl.ds(pl.multiple_of(at * count, count), count), :]
        store(at, last(total))

    if height > 2:

        @pl.loop(1, height - 1)
        def _(at):
            row(at)

    before()
    arrive()
    if height == 1:
        row(0)
    else:

        @pl.loop(0, 2)
        def _(end):
            row(end * (height - 1))


class Edges:
    def __init__(self, groups, rows, count, send, recv):
        self.group, self.me, self.count = lax.axis_index(groups), lax.axis_index(rows), count
        self.send, self.recv = send, recv

    def greet(self, others):
        barrier = pltpu.get_barrier_semaphore()

        def signal(to):
            pl.semaphore_signal(barrier, inc=1, device_id=(self.group, to), device_id_type=pl.DeviceIdType.MESH)

        for other in others:
            signal(other)

        @pl.when(self.me > 0)
        def _():
            signal(self.me - 1)

        @pl.when(self.me < self.count - 1)
        def _():
            signal(self.me + 1)

        inner = (self.me > 0) & (self.me < self.count - 1)

        @pl.when(inner)
        def _():
            pl.semaphore_wait(barrier, 2 + len(others))

        @pl.when(jnp.logical_not(inner))
        def _():
            pl.semaphore_wait(barrier, 1 + len(others))

    def copies(self, buf, height, cells, at):
        def one(source, target, way, step):
            return pltpu.make_async_remote_copy(
                src_ref=buf.at[pl.ds(source * cells, cells)],
                dst_ref=buf.at[pl.ds(target * cells, cells)],
                send_sem=self.send.at[at, way],
                recv_sem=self.recv.at[at, way],
                device_id=(self.group, self.me + step),
                device_id_type=pl.DeviceIdType.MESH,
            )

        return one(1, height + 1, 0, -1), one(height, 0, 1, 1)

    def start(self, buf, height, cells, at):
        up, down = self.copies(buf, height, cells, at)

        @pl.when(self.me > 0)
        def _():
            up.start()

        @pl.when(self.me < self.count - 1)
        def _():
            down.start()

    def arrive(self, buf, height, cells, at):
        up, down = self.copies(buf, height, cells, at)
        zero = jnp.zeros((cells, buf.shape[1]), bf16)

        @pl.when(self.me < self.count - 1)
        def _():
            up.wait_recv()

        @pl.when(self.me == self.count - 1)
        def _():
            buf[(height + 1) * cells : (height + 2) * cells, :] = zero

        @pl.when(self.me > 0)
        def _():
            down.wait_recv()

        @pl.when(self.me == 0)
        def _():
            buf[0:cells, :] = zero

    def sent(self, buf, height, cells, at):
        up, down = self.copies(buf, height, cells, at)

        @pl.when(self.me > 0)
        def _():
            up.wait_send()

        @pl.when(self.me < self.count - 1)
        def _():
            down.wait_send()


class Ring:
    def __init__(self, edges, whole, send, recv, side_send, side_recv):
        self.edges, self.whole = edges, whole
        self.sems = send, recv, side_send, side_recv
        self.chips = edges.count // 2
        self.core = lax.rem(edges.me, 2)
        chip = edges.me // 2
        self.place = jnp.where(lax.rem(chip, 2) == 0, chip // 2, self.chips - 1 - chip // 2)
        self.mate = edges.me + 1 - 2 * self.core
        self.cut = whole.shape[1] // 2

    def at(self, place):
        place = lax.rem(place + 2 * self.chips, self.chips)
        chip = jnp.where(place < self.chips // 2, 2 * place, 2 * (self.chips - 1 - place) + 1)
        return 2 * chip + self.core

    def neighbours(self):
        return [self.at(self.place + 1), self.at(self.place - 1)]

    def copy(self, slot, way, to, send, recv):
        part = self.whole.at[slot, pl.ds(way * self.cut, self.cut)]
        return pltpu.make_async_remote_copy(
            src_ref=part,
            dst_ref=part,
            send_sem=send,
            recv_sem=recv,
            device_id=(self.edges.group, to),
            device_id_type=pl.DeviceIdType.MESH,
        )

    def hop(self, step, way):
        sign = 1 - 2 * way
        send, recv = self.sems[0].at[step, way], self.sems[1].at[step, way]
        return self.copy(self.at(self.place - sign * step), way, self.at(self.place + sign), send, recv)

    def landed(self, step, way):
        sign = 1 - 2 * way
        send, recv = self.sems[0].at[step, way], self.sems[1].at[step, way]
        return self.copy(self.at(self.place - sign * (step + 1)), way, self.at(self.place + sign), send, recv)

    def across(self, step, way, other=False):
        sign = 1 - 2 * way
        slot = self.at(self.place - sign * (step + 1))
        slot = slot + 1 - 2 * self.core if other else slot
        return self.copy(slot, way, self.mate, self.sems[2].at[step + 1, way], self.sems[3].at[step + 1, way])

    def step(self, at):
        if isinstance(at, int) and at >= self.chips:
            return
        for way in range(2):
            if not isinstance(at, int) or at > 0:
                self.landed(at - 1, way).wait_recv()
            if not isinstance(at, int) or at < self.chips - 1:
                self.hop(at, way).start()
            self.across(at - 1, way).start()

    def finish(self, done):
        if done < self.chips:

            @pl.loop(done, self.chips - 1)
            def _(at):
                self.step(at)

            self.step(self.chips - 1)

        @pl.loop(0, self.chips)
        def _(at):
            for way in range(2):
                self.across(at - 1, way, True).wait_recv()

    def sent(self):
        @pl.loop(0, self.chips)
        def _(at):
            for way in range(2):
                self.across(at - 1, way).wait_send()

        @pl.loop(0, self.chips - 1)
        def _(at):
            for way in range(2):
                self.hop(at, way).wait_send()


def into(buf, cells):
    def store(at, value):
        buf[pl.ds(pl.multiple_of((at + 1) * cells, cells), cells), :] = value

    return store


def plain(buf, cells):
    def store(at, value):
        buf[pl.ds(pl.multiple_of(at * cells, cells), cells), :] = value

    return store


def halves(width):
    half = width // 2
    source, target = iota((width, width), 0), iota((width, width), 1)
    return one_hot(source == jnp.where(target < half, 2 * target, 2 * (target - half) + 1))


def weave(width):
    half = width // 2
    source, target = iota((width, width), 0), iota((width, width), 1)
    return one_hot(target == jnp.where(source < half, 2 * source, 2 * (source - half) + 1))


def pool(first, second, chans, parts):
    rows = jnp.maximum(first, second)
    depth, width = rows.shape[0] // chans, rows.shape[1]
    pairs = [
        jnp.maximum(rows[z * chans : (z + 1) * chans], rows[(z + 1) * chans : (z + 2) * chans])
        for z in range(0, depth, 2)
    ]
    split = dot(jnp.concatenate(pairs, axis=0), parts)
    return jnp.maximum(split[:, : width // 2], split[:, width // 2 :]).astype(bf16)


def lift(rows, kernel_ref, ins, outs, woven, store):
    depth = rows.shape[0] // ins
    parts = [dot(kernel_ref[...], rows[z * ins : (z + 1) * ins]).astype(bf16) for z in range(depth)]
    for a in range(2):
        stack = []
        for z in range(depth):
            for b in range(2):
                at = (a * 2 + b) * 2 * outs
                stack.append(jnp.concatenate([parts[z][at : at + outs], parts[z][at + outs : at + 2 * outs]], axis=1))
        store(a, dot(jnp.concatenate(stack, axis=0), woven).astype(bf16))


def network(size, groups, rows, count, *refs):
    (vol, b2, b1, k1, k2, k3, k4, ub, mm, mr, um, fm, fr, out) = refs[:14]
    (b_vol, b_one, b_pool, b_first, e1, e2, e3, e4) = refs[14:22]
    (b_fine, b_mid, b_low, b_bot, bot, b_lift, b_three, four, b_raise, b_last) = refs[22:32]
    (kt, t1, t2, t3a, t3b, t4, t5a, t5b, t6, whole, fine_part, mid_part) = refs[32:44]
    (send, recv, ring_send, ring_recv, side_send, side_recv, local) = refs[44:]
    H, Z, W, C1, C2, C3 = size
    R, R2, RP, RB = Z * C1, Z // 2 * C2, Z // 4 * C2, Z // 4 * C3
    RQ = Z // 2 * C1
    H2, H4 = H // 2, H // 4
    side = C3 // C2
    each = -(-27 // side)
    edges = Edges(groups, rows, count, send, recv)
    ring = Ring(edges, whole, ring_send, ring_recv, side_send, side_recv)
    loads = [
        pltpu.make_async_copy(vol, b_vol.at[pl.ds(R, H * R)], local.at[0]),
        pltpu.make_async_copy(b2, whole.at[edges.me, pl.ds(0, 27)], local.at[1]),
    ]
    for load in loads:
        load.start()
    for t in range(each):
        taps = [b1[q * each + t] if q * each + t < 27 else jnp.zeros(b1.shape[1:], bf16) for q in range(side)]
        whole[edges.me, 27 + t] = jnp.concatenate(taps, axis=-1)
    edges.greet(ring.neighbours())
    loads[0].wait()
    edges.start(b_vol, H, R, 8)
    loads[1].wait()
    ring.step(0)
    band_kernel(e1, k1, C1, C1, C1, 0, Z)
    conv_rows([(e1, b_vol, R)], into(b_one, R), H, R, lambda: edges.arrive(b_vol, H, R, 8), lambda: ring.step(1))
    edges.start(b_one, H, R, 9)
    ring.step(2)
    band_kernel(e2, k2, C1, C1, C1, 0, Z)
    conv_rows([(e2, b_one, R)], into(b_fine, R), H, R, lambda: edges.arrive(b_one, H, R, 9), lambda: ring.step(3))
    parts = halves(W)
    for h in range(H2):
        first, second = b_fine[(2 * h + 1) * R : (2 * h + 2) * R, :], b_fine[(2 * h + 2) * R : (2 * h + 3) * R, :]
        b_pool[(h + 1) * RQ : (h + 2) * RQ, :] = pool(first, second, C1, parts)
    edges.start(b_pool, H2, RQ, 10)
    ring.step(4)
    band_kernel(e3, k3, C2, C1, C1, 0, Z // 2, True)
    conv_rows([(e3, b_pool, RQ)], into(b_first, R2), H2, R2, lambda: edges.arrive(b_pool, H2, RQ, 10))
    edges.start(b_first, H2, R2, 11)
    ring.step(5)
    band_kernel(e4, k4, C2, C2, C2, 0, Z // 2)
    conv_rows([(e4, b_first, R2)], into(b_mid, R2), H2, R2, lambda: edges.arrive(b_first, H2, R2, 11))
    parts = halves(W // 2)
    for h in range(H4):
        first, second = b_mid[(2 * h + 1) * R2 : (2 * h + 2) * R2, :], b_mid[(2 * h + 2) * R2 : (2 * h + 3) * R2, :]
        b_low[(h + 1) * RP : (h + 2) * RP, :] = pool(first, second, C2, parts)
    edges.start(b_low, H4, RP, 0)
    edges.start(b_mid, H2, R2, 1)
    edges.start(b_fine, H, R, 2)
    ring.step(6)
    band_kernel(t5a, fm, C1, 2 * C1, C1, 0, Z)
    conv_rows([(t5a, b_fine, R)], plain(fine_part, R), H, R, lambda: edges.arrive(b_fine, H, R, 2), last=lambda total: total)
    ring.step(7)
    band_kernel(t3a, mm, C2, 2 * C2, C2, 0, Z // 2)
    conv_rows([(t3a, b_mid, R2)], plain(mid_part, R2), H2, R2, lambda: edges.arrive(b_mid, H2, R2, 1), last=lambda total: total)
    band_kernel(t3b, mm, C2, 2 * C2, C2, C2, Z // 2)
    band_kernel(t4, mr, C2, C2, C2, 0, Z // 2)
    band_kernel(t5b, fm, C1, 2 * C1, C1, C1, Z)
    band_kernel(t6, fr, C1, C1, C1, 0, Z)
    ring.finish(8)
    wide = Z // 4 * C2
    shape = (C3, side * wide)
    picks = one_hot(iota(shape, 0) == iota(shape, 1) // wide * C2 + (iota(shape, 1) & (C2 - 1)))
    for t in range(each):
        taps = dot(whole[:, 27 + t].reshape(C3, C3), picks).astype(bf16)
        for q in range(side):
            if q * each + t < 27:
                at = (q * each + t) * C3
                kt[at : at + C3, :] = taps[:, q * wide : (q + 1) * wide]

    def tap(a, b, c):
        at = ((a * 3 + b) * 3 + c) * C3
        return kt[at : at + C3, :].astype(f32)

    band(t1, tap, C3, C2, Z // 4)
    conv_rows([(t1, b_low, RP)], into(b_bot, RB), H4, RB, lambda: edges.arrive(b_low, H4, RP, 0))
    edges.start(b_bot, H4, RB, 3)
    for a in range(3):
        for c in range(3):
            for z in range(Z // 4):
                for y in range(Z // 4):
                    r, l = (c * (Z // 4) + z) * C3, (a * (Z // 4) + y) * C3
                    if -1 <= y - z <= 1:
                        t2[r : r + C3, l : l + C3] = whole[:, (a * 3 + y - z + 1) * 3 + c].reshape(C3, C3)
                    else:
                        t2[r : r + C3, l : l + C3] = jnp.zeros((C3, C3), bf16)
    conv_rows([(t2, b_bot, RB)], plain(bot, RB), H4, RB, lambda: edges.arrive(b_bot, H4, RB, 3))
    woven = weave(W // 2)
    for h in range(H4):

        def store(a, value):
            at = (2 * h + a + 1) * R2
            b_lift[at : at + R2, :] = value

        lift(bot[h * RB : (h + 1) * RB, :], ub, C3, C2, woven, store)
    edges.start(b_lift, H2, R2, 4)
    conv_rows([(t3b, b_lift, R2)], into(b_three, R2), H2, R2, lambda: edges.arrive(b_lift, H2, R2, 4), held=mid_part)
    edges.start(b_three, H2, R2, 5)
    conv_rows([(t4, b_three, R2)], plain(four, R2), H2, R2, lambda: edges.arrive(b_three, H2, R2, 5))
    woven = weave(W)
    for h in range(H2):

        def store(a, value):
            at = (2 * h + a + 1) * R
            b_raise[at : at + R, :] = value

        lift(four[h * R2 : (h + 1) * R2, :], um, C2, C1, woven, store)
    edges.start(b_raise, H, R, 6)
    conv_rows([(t5b, b_raise, R)], into(b_last, R), H, R, lambda: edges.arrive(b_raise, H, R, 6), held=fine_part)
    edges.start(b_last, H, R, 7)
    conv_rows([(t6, b_last, R)], plain(out, R), H, R, lambda: edges.arrive(b_last, H, R, 7))
    for at, (buf, height, cells) in enumerate(
        [(b_low, H4, RP), (b_mid, H2, R2), (b_fine, H, R), (b_bot, H4, RB), (b_lift, H2, R2), (b_three, H2, R2), (b_raise, H, R), (b_last, H, R),
         (b_vol, H, R), (b_one, H, R), (b_pool, H2, RQ), (b_first, H2, R2)]
    ):
        edges.sent(buf, height, cells, at)
    ring.sent()


def per_device(count, *args):
    (volume, f1, f2, m1, m2, b1, b2, ub, mm, mr, um, fm, fr) = args
    C1, H, Z, W = volume.shape
    C2, C3 = m1.shape[3], b2.shape[4]
    own = b1.shape[3]
    R, R2, RP, RL, RB = Z * C1, Z // 2 * C2, Z // 2 * C1, Z // 4 * C2, Z // 4 * C3
    H2, H4, W2, W4 = H // 2, H // 4, W // 2, W // 4
    flat = lambda k: k.reshape(-1, k.shape[-1])
    each = -(-27 // (C3 // C2))
    taps = 27 + each + (27 + each) % 2
    chips = count // 2
    cells = volume.transpose(1, 2, 0, 3).reshape(H * R, W)
    vmem, hbm = pl.BlockSpec(memory_space=pltpu.VMEM), pl.BlockSpec(memory_space=pl.ANY)
    V = lambda *shape: pltpu.VMEM(shape, bf16)
    D = pltpu.SemaphoreType.DMA
    out = pl.pallas_call(
        functools.partial(network, (H, Z, W, C1, C2, C3), "groups", "rows", count),
        out_shape=jax.ShapeDtypeStruct((H * R, W), bf16),
        in_specs=[hbm] * 2 + [vmem] * 11,
        out_specs=vmem,
        scratch_shapes=[
            V((H + 2) * R, W), V((H + 2) * R, W), V((H2 + 2) * RP, W2), V((H2 + 2) * R2, W2),
            V(3 * R, 3 * R), V(3 * R, 3 * R), V(3 * R2, 3 * RP), V(3 * R2, 3 * R2),
            V((H + 2) * R, W), V((H2 + 2) * R2, W2), V((H4 + 2) * RL, W4), V((H4 + 2) * RB, W4), V(H4 * RB, W4),
            V((H2 + 2) * R2, W2), V((H2 + 2) * R2, W2), V(H2 * R2, W2), V((H + 2) * R, W), V((H + 2) * R, W),
            V(27 * C3, Z // 4 * C2), V(3 * RB, 3 * RL), V(3 * RB, 3 * RB), V(3 * R2, 3 * R2), V(3 * R2, 3 * R2),
            V(3 * R2, 3 * R2), V(3 * R, 3 * R), V(3 * R, 3 * R), V(3 * R, 3 * R), V(count, taps, own, C3),
            pltpu.VMEM((H * R, W), f32), pltpu.VMEM((H2 * R2, W2), f32),
            D((12, 2)), D((12, 2)), D((chips - 1, 2)), D((chips - 1, 2)), D((chips, 2)), D((chips, 2)), D((2,)),
        ],
        compiler_params=pltpu.CompilerParams(collective_id=0, has_side_effects=True, vmem_limit_bytes=VMEM_LIMIT),
        name="network",
    )(
        cells, b2.reshape(27, own, C3), b1.reshape(27, own, C2), flat(f1), flat(f2), flat(m1.swapaxes(3, 4)), flat(m2),
        flat(ub), flat(mm), flat(mr), flat(um), flat(fm), flat(fr),
    )
    return out.reshape(H, Z, C1, W).transpose(2, 0, 1, 3)


def solution(mesh):
    placed = [P(None, ("groups", "rows"), None, None)] + [P()] * 12
    placed[5] = placed[6] = P(None, None, None, "rows", None)
    return jax.shard_map(
        functools.partial(per_device, mesh.shape["rows"]),
        mesh=mesh,
        in_specs=tuple(placed),
        out_specs=P(None, ("groups", "rows"), None, None),
        check_vma=False,
    )
```

```python
import functools

import jax
import jax.numpy as jnp
from jax import lax
from jax.experimental import pallas as pl
from jax.experimental.pallas import tpu as pltpu
from jax.sharding import PartitionSpec as P

leakage = 0.01
bf16, f32 = jnp.bfloat16, jnp.float32
VMEM_LIMIT = 56 * 2**20


def iota(shape, axis):
    return lax.broadcasted_iota(jnp.int32, shape, axis)


def one_hot(mask):
    return jnp.where(mask, 1.0, 0.0).astype(bf16)


def dot(a, b):
    return jnp.dot(a, b, preferred_element_type=f32)


def spread(total, channels, offset, copies):
    shape = (total, copies * channels)
    return one_hot((iota(shape, 1) & (channels - 1)) + offset == iota(shape, 0))


def band(target, tap, outs, ins, depth):
    block = iota((outs, depth * ins), 1) // ins
    zero = jnp.zeros((outs, depth * ins), f32)
    for a in range(3):
        for c in range(3):
            taps = [tap(a, b, c) for b in range(3)]
            for z in range(depth):
                rows = zero
                for b in range(3):
                    if 0 <= z + b - 1 < depth:
                        rows = jnp.where(block == z + b - 1, taps[b], rows)
                start = (c * depth + z) * outs
                target[start : start + outs, a * depth * ins : (a + 1) * depth * ins] = rows.astype(bf16)


def band_kernel(target, kernel_ref, outs, total, ins, offset, depth, turned=False):
    picks = spread(total, ins, offset, depth)

    def tap(a, b, c):
        at = (a * 3 + b) * 3 + c
        if turned:
            block = kernel_ref[at * total : (at + 1) * total, :]
            return lax.dot_general(block, picks, (((0,), (0,)), ((), ())), preferred_element_type=f32)
        return dot(kernel_ref[at * outs : (at + 1) * outs, :], picks)

    band(target, tap, outs, ins, depth)


def finish(sums, count):
    width = sums.shape[1]
    lane = iota((count, width), 1)
    left = jnp.where(lane == 0, 0.0, pltpu.roll(sums[:count], 1, 1))
    right = jnp.where(lane == width - 1, 0.0, pltpu.roll(sums[2 * count :], width - 1, 1))
    return left + sums[count : 2 * count] + right


def leaky(total):
    return jnp.maximum(total, leakage * total).astype(bf16)


def conv_rows(sources, store, height, count, arrive, before=lambda: None, held=None, last=leaky):
    def row(at):
        sums = None
        for banded, rows, cells in sources:
            part = dot(banded[...], rows[pl.ds(pl.multiple_of(at * cells, cells), 3 * cells), :])
            sums = part if sums is None else sums + part
        total = finish(sums, count)
        if held is not None:
            total = total + held[pl.ds(pl.multiple_of(at * count, count), count), :]
        store(at, last(total))

    if height > 2:

        @pl.loop(1, height - 1)
        def _(at):
            row(at)

    before()
    arrive()
    if height == 1:
        row(0)
    else:

        @pl.loop(0, 2)
        def _(end):
            row(end * (height - 1))


class Edges:
    def __init__(self, groups, rows, count, send, recv):
        self.group, self.me, self.count = lax.axis_index(groups), lax.axis_index(rows), count
        self.send, self.recv = send, recv

    def greet(self, others):
        barrier = pltpu.get_barrier_semaphore()

        def signal(to):
            pl.semaphore_signal(barrier, inc=1, device_id=(self.group, to), device_id_type=pl.DeviceIdType.MESH)

        for other in others:
            signal(other)

        @pl.when(self.me > 0)
        def _():
            signal(self.me - 1)

        @pl.when(self.me < self.count - 1)
        def _():
            signal(self.me + 1)

        inner = (self.me > 0) & (self.me < self.count - 1)

        @pl.when(inner)
        def _():
            pl.semaphore_wait(barrier, 2 + len(others))

        @pl.when(jnp.logical_not(inner))
        def _():
            pl.semaphore_wait(barrier, 1 + len(others))

    def copies(self, buf, height, cells, at):
        def one(source, target, way, step):
            return pltpu.make_async_remote_copy(
                src_ref=buf.at[pl.ds(source * cells, cells)],
                dst_ref=buf.at[pl.ds(target * cells, cells)],
                send_sem=self.send.at[at, way],
                recv_sem=self.recv.at[at, way],
                device_id=(self.group, self.me + step),
                device_id_type=pl.DeviceIdType.MESH,
            )

        return one(1, height + 1, 0, -1), one(height, 0, 1, 1)

    def start(self, buf, height, cells, at):
        up, down = self.copies(buf, height, cells, at)

        @pl.when(self.me > 0)
        def _():
            up.start()

        @pl.when(self.me < self.count - 1)
        def _():
            down.start()

    def arrive(self, buf, height, cells, at):
        up, down = self.copies(buf, height, cells, at)
        zero = jnp.zeros((cells, buf.shape[1]), bf16)

        @pl.when(self.me < self.count - 1)
        def _():
            up.wait_recv()

        @pl.when(self.me == self.count - 1)
        def _():
            buf[(height + 1) * cells : (height + 2) * cells, :] = zero

        @pl.when(self.me > 0)
        def _():
            down.wait_recv()

        @pl.when(self.me == 0)
        def _():
            buf[0:cells, :] = zero

    def sent(self, buf, height, cells, at):
        up, down = self.copies(buf, height, cells, at)

        @pl.when(self.me > 0)
        def _():
            up.wait_send()

        @pl.when(self.me < self.count - 1)
        def _():
            down.wait_send()


class Ring:
    def __init__(self, edges, whole, send, recv, side_send, side_recv):
        self.edges, self.whole = edges, whole
        self.sems = send, recv, side_send, side_recv
        self.chips = edges.count // 2
        self.core = lax.rem(edges.me, 2)
        chip = edges.me // 2
        self.place = jnp.where(lax.rem(chip, 2) == 0, chip // 2, self.chips - 1 - chip // 2)
        self.mate = edges.me + 1 - 2 * self.core
        self.cut = whole.shape[1] // 2

    def at(self, place):
        place = lax.rem(place + 2 * self.chips, self.chips)
        chip = jnp.where(place < self.chips // 2, 2 * place, 2 * (self.chips - 1 - place) + 1)
        return 2 * chip + self.core

    def neighbours(self):
        return [self.at(self.place + 1), self.at(self.place - 1)]

    def copy(self, slot, way, to, send, recv):
        part = self.whole.at[slot, pl.ds(way * self.cut, self.cut)]
        return pltpu.make_async_remote_copy(
            src_ref=part,
            dst_ref=part,
            send_sem=send,
            recv_sem=recv,
            device_id=(self.edges.group, to),
            device_id_type=pl.DeviceIdType.MESH,
        )

    def hop(self, step, way):
        sign = 1 - 2 * way
        send, recv = self.sems[0].at[step, way], self.sems[1].at[step, way]
        return self.copy(self.at(self.place - sign * step), way, self.at(self.place + sign), send, recv)

    def landed(self, step, way):
        sign = 1 - 2 * way
        send, recv = self.sems[0].at[step, way], self.sems[1].at[step, way]
        return self.copy(self.at(self.place - sign * (step + 1)), way, self.at(self.place + sign), send, recv)

    def across(self, step, way, other=False):
        sign = 1 - 2 * way
        slot = self.at(self.place - sign * (step + 1))
        slot = slot + 1 - 2 * self.core if other else slot
        return self.copy(slot, way, self.mate, self.sems[2].at[step + 1, way], self.sems[3].at[step + 1, way])

    def step(self, at):
        if isinstance(at, int) and at >= self.chips:
            return
        for way in range(2):
            if not isinstance(at, int) or at > 0:
                self.landed(at - 1, way).wait_recv()
            if not isinstance(at, int) or at < self.chips - 1:
                self.hop(at, way).start()
            self.across(at - 1, way).start()

    def finish(self, done):
        if done < self.chips:

            @pl.loop(done, self.chips - 1)
            def _(at):
                self.step(at)

            self.step(self.chips - 1)

        @pl.loop(0, self.chips)
        def _(at):
            for way in range(2):
                self.across(at - 1, way, True).wait_recv()

    def sent(self):
        @pl.loop(0, self.chips)
        def _(at):
            for way in range(2):
                self.across(at - 1, way).wait_send()

        @pl.loop(0, self.chips - 1)
        def _(at):
            for way in range(2):
                self.hop(at, way).wait_send()


def into(buf, cells):
    def store(at, value):
        buf[pl.ds(pl.multiple_of((at + 1) * cells, cells), cells), :] = value

    return store


def plain(buf, cells):
    def store(at, value):
        buf[pl.ds(pl.multiple_of(at * cells, cells), cells), :] = value

    return store


def halves(width):
    half = width // 2
    source, target = iota((width, width), 0), iota((width, width), 1)
    return one_hot(source == jnp.where(target < half, 2 * target, 2 * (target - half) + 1))


def weave(width):
    half = width // 2
    source, target = iota((width, width), 0), iota((width, width), 1)
    return one_hot(target == jnp.where(source < half, 2 * source, 2 * (source - half) + 1))


def pool(first, second, chans, parts):
    rows = jnp.maximum(first, second)
    depth, width = rows.shape[0] // chans, rows.shape[1]
    pairs = [
        jnp.maximum(rows[z * chans : (z + 1) * chans], rows[(z + 1) * chans : (z + 2) * chans])
        for z in range(0, depth, 2)
    ]
    split = dot(jnp.concatenate(pairs, axis=0), parts)
    return jnp.maximum(split[:, : width // 2], split[:, width // 2 :]).astype(bf16)


def lift(rows, kernel_ref, ins, outs, woven, store):
    depth = rows.shape[0] // ins
    parts = [dot(kernel_ref[...], rows[z * ins : (z + 1) * ins]).astype(bf16) for z in range(depth)]
    for a in range(2):
        stack = []
        for z in range(depth):
            for b in range(2):
                at = (a * 2 + b) * 2 * outs
                stack.append(jnp.concatenate([parts[z][at : at + outs], parts[z][at + outs : at + 2 * outs]], axis=1))
        store(a, dot(jnp.concatenate(stack, axis=0), woven).astype(bf16))


def network(size, groups, rows, count, *refs):
    (vol, b2, b1, k1, k2, k3, k4, ub, mm, mr, um, fm, fr, out) = refs[:14]
    (b_vol, b_one, b_pool, b_first, e1, e2, e3, e4) = refs[14:22]
    (b_fine, b_mid, b_low, b_bot, bot, b_lift, b_three, four, b_raise, b_last) = refs[22:32]
    (kt, t1, t2, t3a, t3b, t4, t5a, t5b, t6, whole, fine_part, mid_part) = refs[32:44]
    (send, recv, ring_send, ring_recv, side_send, side_recv, local) = refs[44:]
    H, Z, W, C1, C2, C3 = size
    R, R2, RP, RB = Z * C1, Z // 2 * C2, Z // 4 * C2, Z // 4 * C3
    RQ = Z // 2 * C1
    H2, H4 = H // 2, H // 4
    side = C3 // C2
    each = -(-27 // side)
    edges = Edges(groups, rows, count, send, recv)
    ring = Ring(edges, whole, ring_send, ring_recv, side_send, side_recv)
    loads = [
        pltpu.make_async_copy(vol, b_vol.at[pl.ds(R, H * R)], local.at[0]),
        pltpu.make_async_copy(b2, whole.at[edges.me, pl.ds(0, 27)], local.at[1]),
    ]
    for load in loads:
        load.start()
    for t in range(each):
        taps = [b1[q * each + t] if q * each + t < 27 else jnp.zeros(b1.shape[1:], bf16) for q in range(side)]
        whole[edges.me, 27 + t] = jnp.concatenate(taps, axis=-1)
    edges.greet(ring.neighbours())
    loads[0].wait()
    edges.start(b_vol, H, R, 8)
    loads[1].wait()
    ring.step(0)
    band_kernel(e1, k1, C1, C1, C1, 0, Z)
    conv_rows([(e1, b_vol, R)], into(b_one, R), H, R, lambda: edges.arrive(b_vol, H, R, 8), lambda: ring.step(1))
    edges.start(b_one, H, R, 9)
    ring.step(2)
    band_kernel(e2, k2, C1, C1, C1, 0, Z)
    conv_rows([(e2, b_one, R)], into(b_fine, R), H, R, lambda: edges.arrive(b_one, H, R, 9), lambda: ring.step(3))
    parts = halves(W)
    for h in range(H2):
        first, second = b_fine[(2 * h + 1) * R : (2 * h + 2) * R, :], b_fine[(2 * h + 2) * R : (2 * h + 3) * R, :]
        b_pool[(h + 1) * RQ : (h + 2) * RQ, :] = pool(first, second, C1, parts)
    edges.start(b_pool, H2, RQ, 10)
    ring.step(4)
    band_kernel(e3, k3, C2, C1, C1, 0, Z // 2, True)
    conv_rows([(e3, b_pool, RQ)], into(b_first, R2), H2, R2, lambda: edges.arrive(b_pool, H2, RQ, 10), lambda: ring.step(5))
    edges.start(b_first, H2, R2, 11)
    ring.step(6)
    band_kernel(e4, k4, C2, C2, C2, 0, Z // 2)
    conv_rows([(e4, b_first, R2)], into(b_mid, R2), H2, R2, lambda: edges.arrive(b_first, H2, R2, 11))
    parts = halves(W // 2)
    for h in range(H4):
        first, second = b_mid[(2 * h + 1) * R2 : (2 * h + 2) * R2, :], b_mid[(2 * h + 2) * R2 : (2 * h + 3) * R2, :]
        b_low[(h + 1) * RP : (h + 2) * RP, :] = pool(first, second, C2, parts)
    edges.start(b_low, H4, RP, 0)
    edges.start(b_mid, H2, R2, 1)
    edges.start(b_fine, H, R, 2)
    band_kernel(t5a, fm, C1, 2 * C1, C1, 0, Z)
    conv_rows([(t5a, b_fine, R)], plain(fine_part, R), H, R, lambda: edges.arrive(b_fine, H, R, 2), lambda: ring.step(7), last=lambda total: total)
    band_kernel(t3a, mm, C2, 2 * C2, C2, 0, Z // 2)
    conv_rows([(t3a, b_mid, R2)], plain(mid_part, R2), H2, R2, lambda: edges.arrive(b_mid, H2, R2, 1), last=lambda total: total)
    band_kernel(t3b, mm, C2, 2 * C2, C2, C2, Z // 2)
    band_kernel(t4, mr, C2, C2, C2, 0, Z // 2)
    band_kernel(t5b, fm, C1, 2 * C1, C1, C1, Z)
    band_kernel(t6, fr, C1, C1, C1, 0, Z)
    ring.finish(8)
    wide = Z // 4 * C2
    shape = (C3, side * wide)
    picks = one_hot(iota(shape, 0) == iota(shape, 1) // wide * C2 + (iota(shape, 1) & (C2 - 1)))
    for t in range(each):
        taps = dot(whole[:, 27 + t].reshape(C3, C3), picks).astype(bf16)
        for q in range(side):
            if q * each + t < 27:
                at = (q * each + t) * C3
                kt[at : at + C3, :] = taps[:, q * wide : (q + 1) * wide]

    def tap(a, b, c):
        at = ((a * 3 + b) * 3 + c) * C3
        return kt[at : at + C3, :].astype(f32)

    band(t1, tap, C3, C2, Z // 4)
    conv_rows([(t1, b_low, RP)], into(b_bot, RB), H4, RB, lambda: edges.arrive(b_low, H4, RP, 0))
    edges.start(b_bot, H4, RB, 3)
    for a in range(3):
        for c in range(3):
            for z in range(Z // 4):
                for y in range(Z // 4):
                    r, l = (c * (Z // 4) + z) * C3, (a * (Z // 4) + y) * C3
                    if -1 <= y - z <= 1:
                        t2[r : r + C3, l : l + C3] = whole[:, (a * 3 + y - z + 1) * 3 + c].reshape(C3, C3)
                    else:
                        t2[r : r + C3, l : l + C3] = jnp.zeros((C3, C3), bf16)
    conv_rows([(t2, b_bot, RB)], plain(bot, RB), H4, RB, lambda: edges.arrive(b_bot, H4, RB, 3))
    woven = weave(W // 2)
    for h in range(H4):

        def store(a, value):
            at = (2 * h + a + 1) * R2
            b_lift[at : at + R2, :] = value

        lift(bot[h * RB : (h + 1) * RB, :], ub, C3, C2, woven, store)
    edges.start(b_lift, H2, R2, 4)
    conv_rows([(t3b, b_lift, R2)], into(b_three, R2), H2, R2, lambda: edges.arrive(b_lift, H2, R2, 4), held=mid_part)
    edges.start(b_three, H2, R2, 5)
    conv_rows([(t4, b_three, R2)], plain(four, R2), H2, R2, lambda: edges.arrive(b_three, H2, R2, 5))
    woven = weave(W)
    for h in range(H2):

        def store(a, value):
            at = (2 * h + a + 1) * R
            b_raise[at : at + R, :] = value

        lift(four[h * R2 : (h + 1) * R2, :], um, C2, C1, woven, store)
    edges.start(b_raise, H, R, 6)
    conv_rows([(t5b, b_raise, R)], into(b_last, R), H, R, lambda: edges.arrive(b_raise, H, R, 6), held=fine_part)
    edges.start(b_last, H, R, 7)
    conv_rows([(t6, b_last, R)], plain(out, R), H, R, lambda: edges.arrive(b_last, H, R, 7))
    for at, (buf, height, cells) in enumerate(
        [(b_low, H4, RP), (b_mid, H2, R2), (b_fine, H, R), (b_bot, H4, RB), (b_lift, H2, R2), (b_three, H2, R2), (b_raise, H, R), (b_last, H, R),
         (b_vol, H, R), (b_one, H, R), (b_pool, H2, RQ), (b_first, H2, R2)]
    ):
        edges.sent(buf, height, cells, at)
    ring.sent()


def per_device(count, *args):
    (volume, f1, f2, m1, m2, b1, b2, ub, mm, mr, um, fm, fr) = args
    C1, H, Z, W = volume.shape
    C2, C3 = m1.shape[3], b2.shape[4]
    own = b1.shape[3]
    R, R2, RP, RL, RB = Z * C1, Z // 2 * C2, Z // 2 * C1, Z // 4 * C2, Z // 4 * C3
    H2, H4, W2, W4 = H // 2, H // 4, W // 2, W // 4
    flat = lambda k: k.reshape(-1, k.shape[-1])
    each = -(-27 // (C3 // C2))
    taps = 27 + each + (27 + each) % 2
    chips = count // 2
    cells = volume.transpose(1, 2, 0, 3).reshape(H * R, W)
    vmem, hbm = pl.BlockSpec(memory_space=pltpu.VMEM), pl.BlockSpec(memory_space=pl.ANY)
    V = lambda *shape: pltpu.VMEM(shape, bf16)
    D = pltpu.SemaphoreType.DMA
    out = pl.pallas_call(
        functools.partial(network, (H, Z, W, C1, C2, C3), "groups", "rows", count),
        out_shape=jax.ShapeDtypeStruct((H * R, W), bf16),
        in_specs=[hbm] * 2 + [vmem] * 11,
        out_specs=vmem,
        scratch_shapes=[
            V((H + 2) * R, W), V((H + 2) * R, W), V((H2 + 2) * RP, W2), V((H2 + 2) * R2, W2),
            V(3 * R, 3 * R), V(3 * R, 3 * R), V(3 * R2, 3 * RP), V(3 * R2, 3 * R2),
            V((H + 2) * R, W), V((H2 + 2) * R2, W2), V((H4 + 2) * RL, W4), V((H4 + 2) * RB, W4), V(H4 * RB, W4),
            V((H2 + 2) * R2, W2), V((H2 + 2) * R2, W2), V(H2 * R2, W2), V((H + 2) * R, W), V((H + 2) * R, W),
            V(27 * C3, Z // 4 * C2), V(3 * RB, 3 * RL), V(3 * RB, 3 * RB), V(3 * R2, 3 * R2), V(3 * R2, 3 * R2),
            V(3 * R2, 3 * R2), V(3 * R, 3 * R), V(3 * R, 3 * R), V(3 * R, 3 * R), V(count, taps, own, C3),
            pltpu.VMEM((H * R, W), f32), pltpu.VMEM((H2 * R2, W2), f32),
            D((12, 2)), D((12, 2)), D((chips - 1, 2)), D((chips - 1, 2)), D((chips, 2)), D((chips, 2)), D((2,)),
        ],
        compiler_params=pltpu.CompilerParams(collective_id=0, has_side_effects=True, vmem_limit_bytes=VMEM_LIMIT),
        name="network",
    )(
        cells, b2.reshape(27, own, C3), b1.reshape(27, own, C2), flat(f1), flat(f2), flat(m1.swapaxes(3, 4)), flat(m2),
        flat(ub), flat(mm), flat(mr), flat(um), flat(fm), flat(fr),
    )
    return out.reshape(H, Z, C1, W).transpose(2, 0, 1, 3)


def solution(mesh):
    placed = [P(None, ("groups", "rows"), None, None)] + [P()] * 12
    placed[5] = placed[6] = P(None, None, None, "rows", None)
    return jax.shard_map(
        functools.partial(per_device, mesh.shape["rows"]),
        mesh=mesh,
        in_specs=tuple(placed),
        out_specs=P(None, ("groups", "rows"), None, None),
        check_vma=False,
    )
```
